1024 devices in a mesh: ctx: 16 (over z_lo), exp: 32 (over y, x, core), tp: 2 (over z_hi).
Axes of the slice: x: 4, y: 4, z: 32 (z_hi: 2, z_lo: 16; z = z_hi * 16 + z_lo), core: 2. Of those that a mesh axis runs over, the one named last changes fastest.
Arguments:
- queries: bfloat16 [512, 2, 4, 64, 128], P('ctx', 'tp', None, 'exp'), may hold values from -6 to 6
- keys: bfloat16 [4096, 4, 128], P('ctx'), may hold values from -6 to 6
- values: bfloat16 [4096, 4, 128], P('ctx'), may hold values from -6 to 6
- out_weight: bfloat16 [8192, 4096], P('exp'), may hold values from -0.0625 to 0.0625
- norm_gain: float32 [4096], replicated, may hold values from 0.5 to 1.5
- routes: int32 [4096, 8], P(('ctx', 'exp', 'tp')), may hold values from 0 to 127, as said below
- route_weight: float32 [4096, 8], P(('ctx', 'exp', 'tp')), may hold values from 0.05 to 1
- w_gate: bfloat16 [32, 4096, 384], P('exp', None, 'tp'), may hold values from -0.09375 to 0.09375
- w_up: bfloat16 [32, 4096, 384], P('exp', None, 'tp'), may hold values from -0.09375 to 0.09375
- w_down: bfloat16 [32, 384, 4096], P('exp', 'tp'), may hold values from -0.21875 to 0.21875
Outputs:
- layer_out: bfloat16 [4096, 4096], P(('ctx', 'exp', 'tp'))
The draws below stay inside these ranges and needn't reach their ends.
Inputs may be any that keep to these rules, and one draw needn't show every extreme that they name: `routes`: each row names 8 different experts. In each aligned block of 4 rows no expert is named by more than 2 rows, and some expert is named by exactly 2 rows.
All inputs are finite; a program needn't handle non-finite values.
Results may differ from the reference program's by a relative error of at most 0.025.
Values may be sent and summed in bfloat16 or wider, within the bound.
A program may use at most 32 MiB of HBM per device.

```python
import math
import jax
import jax.numpy as jnp
from jax import lax

D = 4096
HD = 128
KVH = 4
EXPERTS = 128
TOPK = 8
HEAD_DEV = 2
FFW = 768
CAP = 2
ROWS = 4
HEADS = 64
LIVE = 16
QBLOCKS = 512
LEN = 4096
N_EXP = 32
N_TP = 2


def shuffle_row(row_key):
    return jax.random.permutation(row_key, TOPK).astype(jnp.int32)


def draw_routes(key, part):
    live_pick = min(TOPK // 2 - 1, LIVE)
    dead_count = EXPERTS - LIVE
    low_live = min(max(live_pick, -(-(ROWS * live_pick) // CAP)), LIVE)
    high_live = max(low_live, min(LIVE, ROWS * live_pick - 1))
    low_dead = max(TOPK, -(-(ROWS * TOPK) // CAP))

    def one_block(block_key):
        subkeys = jax.random.split(block_key, 7)
        modulus = jax.random.randint(subkeys[0], (), low_live, high_live + 1, dtype=jnp.int32)
        offset = jax.random.randint(subkeys[1], (), 0, modulus, dtype=jnp.int32)
        live_total = jnp.minimum(ROWS * live_pick, CAP * modulus)
        row_ids = jnp.arange(ROWS, dtype=jnp.int32)[:, None]
        col_ids = jnp.arange(TOPK, dtype=jnp.int32)[None, :]
        rank = row_ids * live_pick + col_ids
        is_live = (col_ids < live_pick) & (rank < live_total)
        live_perm = jax.random.permutation(subkeys[2], LIVE).astype(jnp.int32)
        live_ids = live_perm[(offset + rank) % modulus]
        dead_flag = jnp.where(is_live, 0, 1).astype(jnp.int32).reshape(-1)
        inactive_slot_rank = (jnp.cumsum(dead_flag) - 1).astype(jnp.int32).reshape(ROWS, TOPK)
        dead_mod = jax.random.randint(subkeys[3], (), low_dead, dead_count + 1, dtype=jnp.int32)
        dead_off = jax.random.randint(subkeys[4], (), 0, dead_mod, dtype=jnp.int32)
        dead_perm = jax.random.permutation(subkeys[5], dead_count).astype(jnp.int32)
        dead_ids = LIVE + dead_perm[(dead_off + inactive_slot_rank) % dead_mod]
        chosen = jnp.where(is_live, live_ids, dead_ids).astype(jnp.int32)
        orders = jax.vmap(shuffle_row)(jax.random.split(subkeys[6], ROWS))
        return jnp.take_along_axis(chosen, orders, axis=1)
    block_keys = jax.random.split(jax.random.fold_in(key, 7301), LEN // ROWS)
    return jax.vmap(one_block)(block_keys).reshape(LEN, TOPK).astype(jnp.int32)


def block_scale(stream_key, extent, cuts, smallest, high):
    factor_of, own = 1.0, jax.random.fold_in(stream_key, 6)
    for dim, shards_of in cuts:
        heights = jnp.exp(jax.random.uniform(jax.random.fold_in(own, dim), (shards_of,), jnp.float32, smallest / len(cuts), high / len(cuts)))
        factor_of = factor_of * jnp.repeat(heights, extent[dim] // shards_of).reshape([-1 if axis == dim else 1 for axis in range(len(extent))])
    return factor_of


def bell_draw(own_key, extent, spread, most, cuts=(), kind=jnp.bfloat16):
    factor_of = block_scale(own_key, extent, cuts, -0.22, 0.18) if cuts else 1.0
    array = jax.random.normal(own_key, extent, jnp.float32) * spread * factor_of
    return jnp.minimum(jnp.maximum(array, -most), most).astype(kind)


def setup_inputs(seed: int = 0) -> dict:
    key_of = jax.random.split(jax.random.key(seed), 11)
    queries = bell_draw(key_of[0], (QBLOCKS, N_TP, ROWS, HEADS, HD), 1.0, 6.0, ((0, 16), (1, 2), (3, 32)))
    keys = bell_draw(key_of[1], (LEN, KVH, HD), 1.0, 6.0, ((0, 16),))
    values = bell_draw(key_of[2], (LEN, KVH, HD), 1.0, 6.0, ((0, 16),))
    out_weight = bell_draw(key_of[3], (HEADS * HD, D), (HEADS * HD) ** -0.5, 0.0625, ((0, 32),))
    norm_gain = jnp.clip(1.0 + 0.1 * jax.random.normal(key_of[4], (D,), jnp.float32), 0.5, 1.5)
    routes = draw_routes(jax.random.fold_in(key_of[10], 71), 0)
    route_weight = jnp.clip(jnp.exp(math.log(1.0) - 2.9957323 * jax.random.uniform(key_of[6], (LEN, TOPK), jnp.float32) ** block_scale(key_of[6], (LEN, TOPK), ((0, 1024),), -0.2, 0.2)), 0.05, 1.0)
    w_gate = bell_draw(key_of[7], (N_EXP, D, FFW // 2), D ** -0.5, 0.09375, ((0, 32), (2, 2)))
    w_up = bell_draw(key_of[8], (N_EXP, D, FFW // 2), D ** -0.5, 0.09375, ((0, 32), (2, 2)))
    w_down = bell_draw(key_of[9], (N_EXP, FFW // 2, D), FFW ** -0.5, 0.21875, ((0, 32), (1, 2)))
    return {"queries": queries, "keys": keys, "values": values, "out_weight": out_weight, "norm_gain": norm_gain, "routes": routes, "route_weight": route_weight, "w_gate": w_gate, "w_up": w_up, "w_down": w_down}


def silu_mul(gate, up):
    return gate / (1.0 + jnp.exp(-gate)) * up

def block_targets(block_routes, live_count):
    flat = block_routes.reshape(-1)
    order = jnp.arange(flat.shape[0], dtype=jnp.int32)
    same = (flat[:, None] == flat[None, :]) & (order[None, :] < order[:, None])
    slot = lax.optimization_barrier(jnp.sum(same.astype(jnp.int32), axis=1))
    return jnp.where(flat < live_count, flat * CAP + slot, -1)

def reference(queries, keys, values, out_weight, norm_gain, routes, route_weight, w_gate, w_up, w_down):
    heads = HEAD_DEV * N_EXP
    group = heads // KVH
    query_all = queries.reshape(LEN, heads, HD)
    score_scale = HD ** (-0.5)
    position = jnp.arange(LEN, dtype=jnp.int32)
    allowed = position[None, :] <= position[:, None]

    def attend(head):
        query_vector = lax.dynamic_index_in_dim(query_all, head, 1, keepdims=False)
        key = lax.dynamic_index_in_dim(keys, head // group, 1, keepdims=False)
        value = lax.dynamic_index_in_dim(values, head // group, 1, keepdims=False)
        logit_score = jnp.dot(query_vector, key.T, preferred_element_type=jnp.float32) * score_scale
        logit_score = jnp.where(allowed, logit_score, -1e+30)
        highest = lax.optimization_barrier(jnp.max(logit_score, axis=1, keepdims=True))
        attention_probability = jnp.where(allowed, jnp.exp(logit_score - highest), 0.0)
        total = lax.optimization_barrier(jnp.sum(attention_probability, axis=1, keepdims=True))
        mixed = jnp.dot(attention_probability.astype(jnp.bfloat16), value, preferred_element_type=jnp.float32)
        return (mixed / total).astype(jnp.bfloat16)
    attended = lax.map(attend, jnp.arange(heads, dtype=jnp.int32))
    per_group = attended.reshape(N_EXP, HEAD_DEV, LEN, HD).transpose(0, 2, 1, 3).reshape(N_EXP, LEN, HEAD_DEV * HD)
    weight_groups = out_weight.reshape(N_EXP, HEAD_DEV * HD, D)

    def add_group(total, pair):
        group_rows, weight = pair
        term = jnp.dot(group_rows, weight, preferred_element_type=jnp.float32).astype(jnp.bfloat16)
        term = lax.optimization_barrier(term)
        return (total + term.astype(jnp.float32), None)
    summed, _ = lax.scan(add_group, jnp.zeros((LEN, D), jnp.float32), (per_group, weight_groups))
    state = summed.astype(jnp.bfloat16)
    state_wide = state.astype(jnp.float32)
    inverse = lax.rsqrt(lax.optimization_barrier(jnp.mean(state_wide * state_wide, axis=1, keepdims=True)) + 1e-06)
    normed = (state_wide * inverse * norm_gain.astype(jnp.float32)[None, :]).astype(jnp.bfloat16)
    live_count = N_EXP // 2
    blocks = LEN // ROWS
    normed_blocks = normed.reshape(blocks, ROWS, D)
    route_blocks = routes.reshape(blocks, ROWS, TOPK)
    weight_blocks = route_weight.reshape(blocks, ROWS, TOPK)

    def build(block_routes, block_rows, block_weight):
        target = block_targets(block_routes, live_count)
        slots = jnp.arange(live_count * CAP, dtype=jnp.int32)
        hit = (target[None, :] == slots[:, None]).astype(jnp.float32).reshape(live_count * CAP, ROWS, TOPK)
        pick = lax.optimization_barrier(jnp.sum(hit, axis=2)).astype(jnp.bfloat16)
        buffer = jnp.dot(pick, block_rows, preferred_element_type=jnp.float32).astype(jnp.bfloat16)
        share = block_weight / lax.optimization_barrier(jnp.sum(block_weight, axis=1, keepdims=True))
        mix = lax.optimization_barrier(jnp.sum(hit * share[None, :, :], axis=2)).T
        return (buffer.reshape(live_count, CAP, D), mix)
    buffers, mixes = jax.vmap(build)(route_blocks, normed_blocks, weight_blocks)
    part = FFW // (2 * N_TP)

    def expert(total, index):
        expert_rows = lax.dynamic_index_in_dim(buffers, index, 1, keepdims=False).reshape(blocks * CAP, D)
        result = jnp.zeros((blocks * CAP, D), jnp.float32)
        for half in range(2):
            gate_all = lax.dynamic_index_in_dim(w_gate, half * live_count + index, 0, keepdims=False)
            up_all = lax.dynamic_index_in_dim(w_up, half * live_count + index, 0, keepdims=False)
            down_all = lax.dynamic_index_in_dim(w_down, half * live_count + index, 0, keepdims=False)
            for lane in range(N_TP):
                gate = jnp.dot(expert_rows, gate_all[:, lane * part:(lane + 1) * part], preferred_element_type=jnp.float32)
                up = jnp.dot(expert_rows, up_all[:, lane * part:(lane + 1) * part], preferred_element_type=jnp.float32)
                hidden = silu_mul(gate, up).astype(jnp.bfloat16)
                piece = jnp.dot(hidden, down_all[lane * part:(lane + 1) * part, :], preferred_element_type=jnp.float32).astype(jnp.bfloat16)
                piece = lax.optimization_barrier(piece)
                result = result + piece.astype(jnp.float32)
        mix_part = lax.dynamic_slice_in_dim(mixes, index * CAP, CAP, 2)
        contrib = jnp.einsum('brc,bcd->brd', mix_part, result.reshape(blocks, CAP, D), precision=lax.Precision.HIGHEST)
        return (total + contrib, None)
    moe, _ = lax.scan(expert, jnp.zeros((blocks, ROWS, D), jnp.float32), jnp.arange(live_count, dtype=jnp.int32))
    return (state_wide + moe.reshape(LEN, D)).astype(jnp.bfloat16)
```

```python
import functools
import jax
import jax.numpy as jnp
from jax import lax
from jax.experimental import pallas as pl
from jax.experimental.pallas import tpu as pltpu
from jax.sharding import PartitionSpec as P

MESH = pl.DeviceIdType.MESH
VMEM = pltpu.VMEM
F32 = jnp.float32
BF16 = jnp.bfloat16
CHUNK = 256
HALF = 128
NC = 16


def where_am_i():
    c = lax.axis_index("ctx")
    e = lax.axis_index("exp")
    t = lax.axis_index("tp")
    return t * NC + c, e // 8, lax.rem(e // 2, 4), lax.rem(e, 2)


def device(z, y, x, k):
    z = lax.rem(z + 2 * NC, 2 * NC)
    y = lax.rem(y + 4, 4)
    x = lax.rem(x + 4, 4)
    return (lax.rem(z, NC), (y * 4 + x) * 2 + k, z // NC)


def greet(devices):
    barrier = pltpu.get_barrier_semaphore()
    for d in devices:
        pl.semaphore_signal(barrier, inc=1, device_id=d, device_id_type=MESH)
    pl.semaphore_wait(barrier, len(devices))


def remote(src, dst, ssem, rsem, dev):
    return pltpu.make_async_remote_copy(
        src_ref=src, dst_ref=dst, send_sem=ssem, recv_sem=rsem, device_id=dev, device_id_type=MESH
    )


def attention_kernel(q_ref, mine_ref, o_ref, kv, up_s, up_r, dn_s, dn_r, x_s, x_r, c_s, c_r):
    z, y, x, k = where_am_i()
    c = lax.axis_index("ctx")
    t = lax.axis_index("tp")
    half = lax.rem(x, 2)
    up1, up2 = device(z + 1, y, x, k), device(z + 2, y, x, k)
    dn1, dn2 = device(z - 1, y, x, k), device(z - 2, y, x, k)
    beside = device(z, y, x + 1 - 2 * half, k)
    other = device(z, y, x, 1 - k)
    greet([up1, up2, dn1, dn2, beside, other])

    own = mine_ref.at[k, pl.ds(half * HALF, HALF)]

    def piece(pos):
        return kv.at[k, pos, half]

    def up_copy(p, src, dev):
        return remote(src, piece(2 * p), up_s.at[p], up_r.at[p], dev)

    def dn_copy(p, src, dev):
        return remote(src, piece(2 * p + 1), dn_s.at[p], dn_r.at[p], dev)

    def width(p):
        return 2 if p < 7 else 1

    def x_copy(p):
        blk = kv.at[k, pl.ds(2 * p, width(p)), half]
        return remote(blk, blk, x_s.at[p], x_r.at[p], beside)

    def c_copy(p):
        blk = kv.at[k, pl.ds(2 * p, width(p))]
        return remote(blk, blk, c_s.at[p], c_r.at[p], other)

    ups = [up_copy(0, own, up1), up_copy(1, own, up2)]
    dns = [dn_copy(0, own, dn1), dn_copy(1, own, dn2)]
    for p in range(2, 8):
        ups.append(up_copy(p, piece(2 * p - 4), up2))
    for p in range(2, 7):
        dns.append(dn_copy(p, piece(2 * p - 3), dn2))
    xs = [x_copy(p) for p in range(8)]
    cs = [c_copy(p) for p in range(8)]
    ups[0].start()
    dns[0].start()
    ups[1].start()
    dns[1].start()

    scale = 128 ** (-0.5)
    q = q_ref[...].reshape(256, 128)

    def scores(keys):
        return lax.dot_general(q, keys, (((1,), (1,)), ((), ())), preferred_element_type=F32) * scale

    def mix(prob, vals):
        return jnp.dot(prob.astype(BF16), vals, preferred_element_type=F32)

    s = scores(mine_ref[0])
    row = lax.broadcasted_iota(jnp.int32, (256, CHUNK), 0) & 127
    col = lax.broadcasted_iota(jnp.int32, (256, CHUNK), 1)
    pos = ((row >> 2) * 2 + t) * 4 + (row & 3)
    ok = col <= pos
    s = jnp.where(ok, s, -1e30)
    m = jnp.max(s, axis=1, keepdims=True)
    e = jnp.where(ok, jnp.exp(s - m), 0.0)
    l = jnp.sum(e, axis=1, keepdims=True)
    acc = mix(e, mine_ref[1])

    def z_stage(p):
        ups[p].wait_recv()
        if p + 2 < 8:
            ups[p + 2].start()
        if p < 7:
            dns[p].wait_recv()
            if p + 2 < 7:
                dns[p + 2].start()
        xs[p].start()

    def x_stage(p):
        xs[p].wait_recv()
        cs[p].start()

    def absorb(p, m, l, acc):
        cs[p].wait_recv()
        n = width(p)
        keys = kv[0, pl.ds(2 * p, n)].reshape(n * CHUNK, 128)
        vals = kv[1, pl.ds(2 * p, n)].reshape(n * CHUNK, 128)
        off = p + 1
        seen_up = c >= off
        seen_dn = c + off >= NC
        s = scores(keys)
        lane = lax.broadcasted_iota(jnp.int32, (1, n * CHUNK), 1)
        bias_up = jnp.where(seen_up, 0.0, -1e30)
        bias_dn = jnp.where(seen_dn, 0.0, -1e30)
        s = s + jnp.where(lane < CHUNK, bias_up, bias_dn)
        m_new = jnp.maximum(m, jnp.max(s, axis=1, keepdims=True))
        fade = jnp.exp(m - m_new)
        e = jnp.exp(s - m_new)
        return m_new, l * fade + jnp.sum(e, axis=1, keepdims=True), acc * fade + mix(e, vals)

    for i in range(8 + 2):
        if i < 8:
            z_stage(i)
        if 0 <= i - 1 < 8:
            x_stage(i - 1)
        if 0 <= i - 2 < 8:
            m, l, acc = absorb(i - 2, m, l, acc)
    out = (acc / l).astype(BF16)
    o_ref[:, 0:128] = out[0:128]
    o_ref[:, 128:256] = out[128:256]
    for cp in ups + dns + xs + cs:
        cp.wait_send()


def attention(q, mine):
    dma = pltpu.SemaphoreType.DMA
    return pl.pallas_call(
        attention_kernel,
        out_shape=jax.ShapeDtypeStruct((128, 256), BF16),
        in_specs=[pl.BlockSpec(memory_space=VMEM)] * 2,
        out_specs=pl.BlockSpec(memory_space=VMEM),
        scratch_shapes=[VMEM((2, 16, 2, HALF, 128), BF16)] + [dma((8,))] * 8,
        compiler_params=pltpu.CompilerParams(collective_id=0, has_side_effects=True),
        name="gather_attend",
    )(q, mine)


CAP = 2


def split_up(shard, dim, length):
    before, after = (shard.shape[:dim], shard.shape[dim + 1 :])
    return jnp.moveaxis(shard.reshape(*before, length, -1, *after), dim, 0)


def sum_at_owner(shard, axis, dim):
    length = lax.axis_size(axis)
    pieces = lax.all_to_all(split_up(shard, dim, length), axis, 0, 0, tiled=True)
    return jnp.sum(pieces.astype(jnp.float32), axis=0)


def silu_mul(gate, up):
    return gate / (1.0 + jnp.exp(-gate)) * up


def on_device(
    queries, keys, values, out_weight, norm_gain, routes, route_weight, w_gate, w_up, w_down
):
    blocks, lanes, rows, local_heads, head_dim = queries.shape
    width = out_weight.shape[1]
    n_exp = lax.axis_size("exp")
    n_tp = lax.axis_size("tp")
    live_count = n_exp // 2
    ctx_index = lax.axis_index("ctx")
    exp_index = lax.axis_index("exp")
    tp_index = lax.axis_index("tp")
    group = local_heads * n_exp // keys.shape[1]
    kv_head = exp_index * local_heads // group
    mine = jnp.stack(
        [
            lax.dynamic_index_in_dim(keys, kv_head, 1, keepdims=False),
            lax.dynamic_index_in_dim(values, kv_head, 1, keepdims=False),
        ]
    )
    query_rows = blocks * rows
    query_vector = queries.reshape(query_rows, local_heads, head_dim).transpose(1, 0, 2)
    mixed_rows = attention(query_vector, mine)
    summed = sum_at_owner(
        jnp.dot(mixed_rows, out_weight, preferred_element_type=jnp.float32).astype(jnp.bfloat16),
        "exp",
        0,
    )
    state = summed.astype(jnp.bfloat16)
    state_wide = state.astype(jnp.float32)
    inverse = lax.rsqrt(jnp.mean(state_wide * state_wide, axis=1, keepdims=True) + 1e-06)
    normed = (state_wide * inverse * norm_gain[None, :]).astype(jnp.bfloat16)
    picks = routes.shape[1]
    flat = routes.reshape(-1)
    order = jnp.arange(flat.shape[0], dtype=jnp.int32)
    same = (flat[:, None] == flat[None, :]) & (order[None, :] < order[:, None])
    slot = jnp.sum(same.astype(jnp.int32), axis=1)
    target = jnp.where(flat < live_count, flat * CAP + slot, -1)
    slots = jnp.arange(live_count * CAP, dtype=jnp.int32)
    hit = (
        (target[None, :] == slots[:, None])
        .astype(jnp.float32)
        .reshape(live_count * CAP, rows, picks)
    )
    pick = jnp.sum(hit, axis=2).astype(jnp.bfloat16)
    buffer = (
        jnp.dot(pick, normed, preferred_element_type=jnp.float32)
        .astype(jnp.bfloat16)
        .reshape(live_count, CAP, width)
    )
    share = route_weight / jnp.sum(route_weight, axis=1, keepdims=True)
    mix = jnp.sum(hit * share[None, :, :], axis=2).T
    outgoing = jnp.broadcast_to(buffer[None, :, None], (2, live_count, n_tp, CAP, width)).reshape(
        n_exp * n_tp, CAP, width
    )
    received = lax.all_to_all(outgoing, ("exp", "tp"), split_axis=0, concat_axis=0, tiled=True)
    flat_rows = received.reshape(-1, width)
    gate = jnp.dot(flat_rows, w_gate[0], preferred_element_type=jnp.float32)
    up = jnp.dot(flat_rows, w_up[0], preferred_element_type=jnp.float32)
    hidden = silu_mul(gate, up).astype(jnp.bfloat16)
    result = jnp.dot(hidden, w_down[0], preferred_element_type=jnp.float32).astype(jnp.bfloat16)
    returned = lax.all_to_all(
        result.reshape(received.shape), ("exp", "tp"), split_axis=0, concat_axis=0, tiled=True
    )
    expert_output_rows = jnp.sum(
        returned.astype(jnp.float32).reshape(2, live_count, n_tp, CAP, width), axis=(0, 2)
    )
    moe = jnp.dot(
        mix, expert_output_rows.reshape(live_count * CAP, width), preferred_element_type=jnp.float32
    )
    return (state_wide + moe).astype(jnp.bfloat16)


def solution(mesh):
    in_specs = (
        P("ctx", "tp", None, "exp", None),
        P("ctx", None, None),
        P("ctx", None, None),
        P("exp", None),
        P(),
        P(("ctx", "exp", "tp"), None),
        P(("ctx", "exp", "tp"), None),
        P("exp", None, "tp"),
        P("exp", None, "tp"),
        P("exp", "tp", None),
    )
    out_specs = P(("ctx", "exp", "tp"), None)
    return jax.shard_map(
        on_device, mesh=mesh, in_specs=in_specs, out_specs=out_specs, check_vma=False
    )
```

```python
import functools
import jax
import jax.numpy as jnp
from jax import lax
from jax.experimental import pallas as pl
from jax.experimental.pallas import tpu as pltpu
from jax.sharding import PartitionSpec as P

MESH = pl.DeviceIdType.MESH
VMEM = pltpu.VMEM
F32 = jnp.float32
BF16 = jnp.bfloat16
CHUNK = 256
HALF = 128
NC = 16


def where_am_i():
    c = lax.axis_index("ctx")
    e = lax.axis_index("exp")
    t = lax.axis_index("tp")
    return t * NC + c, e // 8, lax.rem(e // 2, 4), lax.rem(e, 2)


def device(z, y, x, k):
    z = lax.rem(z + 2 * NC, 2 * NC)
    y = lax.rem(y + 4, 4)
    x = lax.rem(x + 4, 4)
    return (lax.rem(z, NC), (y * 4 + x) * 2 + k, z // NC)


def greet(devices):
    barrier = pltpu.get_barrier_semaphore()
    for d in devices:
        pl.semaphore_signal(barrier, inc=1, device_id=d, device_id_type=MESH)
    pl.semaphore_wait(barrier, len(devices))


def remote(src, dst, ssem, rsem, dev):
    return pltpu.make_async_remote_copy(
        src_ref=src, dst_ref=dst, send_sem=ssem, recv_sem=rsem, device_id=dev, device_id_type=MESH
    )


def attention_kernel(q_ref, mine_ref, o_ref, kv, up_s, up_r, dn_s, dn_r, x_s, x_r, c_s, c_r):
    z, y, x, k = where_am_i()
    c = lax.axis_index("ctx")
    t = lax.axis_index("tp")
    half = lax.rem(x, 2)
    up1, up2 = device(z + 1, y, x, k), device(z + 2, y, x, k)
    dn1, dn2 = device(z - 1, y, x, k), device(z - 2, y, x, k)
    beside = device(z, y, x + 1 - 2 * half, k)
    other = device(z, y, x, 1 - k)
    greet([up1, up2, dn1, dn2, beside, other])

    own = mine_ref.at[k, pl.ds(half * HALF, HALF)]

    def piece(pos):
        return kv.at[k, pos, half]

    def up_copy(p, src, dev):
        return remote(src, piece(2 * p), up_s.at[p], up_r.at[p], dev)

    def dn_copy(p, src, dev):
        return remote(src, piece(2 * p + 1), dn_s.at[p], dn_r.at[p], dev)

    def width(p):
        return 2 if p < 7 else 1

    def x_copy(p):
        blk = kv.at[k, pl.ds(2 * p, width(p)), half]
        return remote(blk, blk, x_s.at[p], x_r.at[p], beside)

    def c_copy(p):
        blk = kv.at[k, pl.ds(2 * p, width(p))]
        return remote(blk, blk, c_s.at[p], c_r.at[p], other)

    ups = [up_copy(0, own, up1), up_copy(1, own, up2)]
    dns = [dn_copy(0, own, dn1), dn_copy(1, own, dn2)]
    for p in range(2, 8):
        ups.append(up_copy(p, piece(2 * p - 4), up2))
    for p in range(2, 7):
        dns.append(dn_copy(p, piece(2 * p - 3), dn2))
    xs = [x_copy(p) for p in range(8)]
    cs = [c_copy(p) for p in range(8)]
    ups[0].start()
    dns[0].start()
    ups[1].start()
    dns[1].start()

    scale = 128 ** (-0.5)
    q = q_ref[...].reshape(256, 128)

    def scores(keys):
        return lax.dot_general(q, keys, (((1,), (1,)), ((), ())), preferred_element_type=F32) * scale

    def mix(prob, vals):
        return jnp.dot(prob.astype(BF16), vals, preferred_element_type=F32)

    s = scores(mine_ref[0])
    row = lax.broadcasted_iota(jnp.int32, (256, CHUNK), 0) & 127
    col = lax.broadcasted_iota(jnp.int32, (256, CHUNK), 1)
    pos = ((row >> 2) * 2 + t) * 4 + (row & 3)
    ok = col <= pos
    s = jnp.where(ok, s, -1e30)
    m = jnp.max(s, axis=1, keepdims=True)
    e = jnp.where(ok, jnp.exp(s - m), 0.0)
    l = jnp.sum(e, axis=1, keepdims=True)
    acc = mix(e, mine_ref[1])

    def z_stage(p):
        ups[p].wait_recv()
        if p + 2 < 8:
            ups[p + 2].start()
        if p < 7:
            dns[p].wait_recv()
            if p + 2 < 7:
                dns[p + 2].start()
        xs[p].start()

    def x_stage(p):
        xs[p].wait_recv()
        cs[p].start()

    def absorb(p, m, l, acc):
        cs[p].wait_recv()
        n = width(p)
        keys = kv[0, pl.ds(2 * p, n)].reshape(n * CHUNK, 128)
        vals = kv[1, pl.ds(2 * p, n)].reshape(n * CHUNK, 128)
        off = p + 1
        seen_up = c >= off
        seen_dn = c + off >= NC
        s = scores(keys)
        lane = lax.broadcasted_iota(jnp.int32, (1, n * CHUNK), 1)
        bias_up = jnp.where(seen_up, 0.0, -1e30)
        bias_dn = jnp.where(seen_dn, 0.0, -1e30)
        s = s + jnp.where(lane < CHUNK, bias_up, bias_dn)
        m_new = jnp.maximum(m, jnp.max(s, axis=1, keepdims=True))
        fade = jnp.exp(m - m_new)
        e = jnp.exp(s - m_new)
        return m_new, l * fade + jnp.sum(e, axis=1, keepdims=True), acc * fade + mix(e, vals)

    for i in range(8 + 2):
        if i < 8:
            z_stage(i)
        if 0 <= i - 1 < 8:
            x_stage(i - 1)
        if 0 <= i - 2 < 8:
            m, l, acc = absorb(i - 2, m, l, acc)
    out = (acc / l).astype(BF16)
    o_ref[:, 0:128] = out[0:128]
    o_ref[:, 128:256] = out[128:256]
    for cp in ups + dns + xs + cs:
        cp.wait_send()


def attention(q, mine):
    dma = pltpu.SemaphoreType.DMA
    return pl.pallas_call(
        attention_kernel,
        out_shape=jax.ShapeDtypeStruct((128, 256), BF16),
        in_specs=[pl.BlockSpec(memory_space=VMEM)] * 2,
        out_specs=pl.BlockSpec(memory_space=VMEM),
        scratch_shapes=[VMEM((2, 16, 2, HALF, 128), BF16)] + [dma((8,))] * 8,
        compiler_params=pltpu.CompilerParams(collective_id=0, has_side_effects=True),
        name="gather_attend",
    )(q, mine)


WIDE = 4096
HC = 2048
MSG = HC + 128
FF = 192
COLS = 512
PARTS = HC // COLS


def experts_kernel(
    mixed_ref, gain_ref, meta_ref, wo_hbm, wg_hbm, wu_hbm, wd_hbm, out_ref,
    wo, wg, wu, wd, xb, acc, keep, s0, r0, s1, r1, s2, r2, xs, xr, fs, fr, hid,
    w_sem, b_s, b_r, a_s, a_r, c_s, c_r, m_s, m_r, n_s, n_r, l_s, l_r, z_s, z_r, f_s, f_r,
):
    z, y, x, k = where_am_i()
    a = x * (1 - k) + y * k
    o = y * (1 - k) + x * k
    other = device(z, y, x, 1 - k)
    to_a = [None] + [device(z, y + r * k, x + r * (1 - k), k) for r in (1, 2, 3)]
    to_b = [None] + [device(z, y + r * (1 - k), x + r * k, k) for r in (1, 2, 3)]
    far = device(z + jnp.where(lax.rem(z // 8, 2) == 1, 8, -8), y, x, k)

    def block(aa, oo):
        aa, oo = lax.rem(aa + 4, 4), lax.rem(oo + 4, 4)
        return oo * (4 - 3 * k) + aa * (1 + 3 * k)

    me = block(a, o)
    loads = [
        pltpu.make_async_copy(src, dst, w_sem.at[i])
        for i, (src, dst) in enumerate(
            ((wo_hbm, wo), (wg_hbm.at[0], wg), (wu_hbm.at[0], wu), (wd_hbm.at[0], wd))
        )
    ]
    for cp in loads:
        cp.start()
    sent = []

    def go(cp):
        cp.start()
        sent.append(cp)

    peers = [other, far] + to_a[1:] + to_b[1:]
    barrier = pltpu.get_barrier_semaphore()
    for d in peers:
        pl.semaphore_signal(barrier, inc=1, device_id=d, device_id_type=MESH)

    def rs_pair(i, j):
        cols = pl.ds(j * COLS, COLS)
        return remote(s0.at[i, :, :, cols], r0.at[i, :, :, cols], l_s.at[i, j], l_r.at[i, j], other)

    def rs_a(i, r):
        return remote(s1.at[i, r - 1], r1.at[i, r - 1], m_s.at[i, r - 1], m_r.at[i, r - 1], to_a[r])

    def rs_b(i, r):
        return remote(s2.at[i, r - 1], r2.at[i, r - 1], n_s.at[i, r - 1], n_r.at[i, r - 1], to_b[r])

    def times(lhs, w, half, j):
        cols = pl.ds(pl.multiple_of(half * HC + j * COLS, COLS), COLS)
        return jnp.dot(lhs, w[:, cols], preferred_element_type=F32).reshape(16, 8, COLS)

    def rs_pair_fill(i, lhs, w):
        for j in range(PARTS):
            s0[i, :, :, j * COLS:(j + 1) * COLS] = times(lhs, w, 1 - k, j).astype(BF16)

    def rs_pair_go(i):
        for j in range(PARTS):
            go(rs_pair(i, j))

    def rs_own(lhs, w):
        for j in range(PARTS):
            acc[:, :, j * COLS:(j + 1) * COLS] = times(lhs, w, k, j)

    def rs_first(i):
        for j in range(PARTS):
            rs_pair(i, j).wait_recv()
        for r in (2, 1, 3, 0):
            for oo in range(4):
                b = block(a + r, oo)
                v = acc[b] + r0[i, b].astype(F32)
                if r:
                    s1[i, r - 1, oo] = v.astype(BF16)
                else:
                    keep[oo] = v
            if r:
                go(rs_a(i, r))

    def rs_second(i):
        for r in (1, 3, 2):
            rs_a(i, r).wait_recv()
        for r in (2, 1, 3, 0):
            oo = lax.rem(o + r, 4)
            v = keep[oo]
            for q in range(3):
                v = v + r1[i, q, oo].astype(F32)
            if r:
                s2[i, r - 1] = v.astype(BF16)
                go(rs_b(i, r))
        return v

    def rs_last(i, v):
        for r in (1, 3, 2):
            rs_b(i, r).wait_recv()
        for q in range(3):
            v = v + r2[i, q].astype(F32)
        return v

    def ag_b(p, r):
        blk = xb.at[p, k, me]
        return remote(blk, blk, b_s.at[p, r - 1], b_r.at[p, r - 1], to_b[r])

    def ag_a(p, q, r):
        blk = xb.at[p, k, block(a, o - q)]
        return remote(blk, blk, a_s.at[p, q, r - 1], a_r.at[p, q, r - 1], to_a[r])

    def ag_c(p, q, r):
        blk = xb.at[p, k, block(a - r, o - q)]
        return remote(blk, blk, c_s.at[p, q, r], c_r.at[p, q, r], other)

    def ag_start(p):
        for r in (2, 1, 3):
            go(ag_b(p, r))
        for r in (2, 1, 3):
            go(ag_a(p, 0, r))
        go(ag_c(p, 0, 0))

    def ag_forward(p):
        for q in (1, 3, 2):
            ag_b(p, q).wait_recv()
            for r in (2, 1, 3):
                go(ag_a(p, q, r))
            go(ag_c(p, q, 0))

    def ag_pair(p):
        for q in (0, 1, 3, 2):
            for r in (1, 3, 2):
                ag_a(p, q, r).wait_recv()
                go(ag_c(p, q, r))

    def ag_wait(p):
        for q in range(4):
            for r in range(4):
                ag_c(p, q, r).wait_recv()

    lane = lax.broadcasted_iota(jnp.int32, (1, 128), 1)
    expert = lax.rem((y * 4 + x) * 2 + k, 16)

    def ffn(p):
        info = xb[p, 0, :, :, HC:MSG].astype(F32) + xb[p, 1, :, :, HC:MSG].astype(F32)
        info = info.reshape(128, 128)
        square = jnp.sum(jnp.where(lane < 16, info, 0.0), axis=1, keepdims=True)
        mine = (lane == 16 + expert) | (lane == 32 + expert)
        share = jnp.sum(jnp.where(mine, info, 0.0), axis=1, keepdims=True)
        inverse = lax.rsqrt(square * (1.0 / WIDE) + 1e-06)
        gate = jnp.zeros((128, FF), F32)
        up = jnp.zeros((128, FF), F32)
        for h in range(2):
            for j in range(PARTS):
                v = xb[p, h, :, :, j * COLS:(j + 1) * COLS].astype(F32).reshape(128, COLS)
                at = h * HC + j * COLS
                v = (v * inverse * gain_ref[:, at:at + COLS]).astype(BF16)
                gate += jnp.dot(v, wg[at:at + COLS], preferred_element_type=F32)
                up += jnp.dot(v, wu[at:at + COLS], preferred_element_type=F32)
        return (gate / (1.0 + jnp.exp(-gate)) * up * share).astype(BF16)

    mixed = mixed_ref[...]
    loads[0].wait()
    rs_pair_fill(0, mixed, wo)
    pl.semaphore_wait(barrier, len(peers))
    rs_pair_go(0)
    rs_own(mixed, wo)
    rs_first(0)
    state = rs_last(0, rs_second(0)).astype(BF16)
    state_wide = state.astype(F32)
    square = jnp.sum(state_wide * state_wide, axis=1, keepdims=True)
    top = square.astype(BF16).astype(F32)
    mid = (square - top).astype(BF16).astype(F32)
    meta = meta_ref[...]
    high = meta.astype(BF16).astype(F32)
    info = jnp.where(lane < 32, high, meta - high)
    info = jnp.where(lane == 0, top, info)
    info = jnp.where(lane == 1, mid, info)
    info = jnp.where(lane == 2, square - top - mid, info)
    xb[0, k, me, :, 0:HC] = state
    xb[0, k, me, :, HC:MSG] = info.astype(BF16)
    cross = remote(xb.at[0, k, me], xb.at[1, k, me], z_s.at[0], z_r.at[0], far)
    go(cross)
    ag_start(0)
    ag_forward(0)
    ag_pair(0)
    for cp in loads[1:]:
        cp.wait()
    ag_wait(0)
    hid[...] = ffn(0)
    cross.wait_recv()
    ag_start(1)
    ag_forward(1)
    ag_pair(1)
    ag_wait(1)
    hidden = ffn(1)
    rs_pair_fill(1, hidden, wd)
    rs_pair_go(1)
    rs_own(hidden, wd)
    rs_first(1)
    xs[...] = rs_last(1, rs_second(1)).astype(BF16)
    back = remote(xs, xr, z_s.at[1], z_r.at[1], far)
    go(back)
    hidden = hid[...]
    rs_pair_fill(2, hidden, wd)
    rs_pair_go(2)
    rs_own(hidden, wd)
    rs_first(2)
    moe = rs_last(2, rs_second(2))
    back.wait_recv()
    total = (state_wide + moe + xr[...].astype(F32)).astype(BF16).astype(F32)
    low, upper = total[0:4], total[4:8]
    fs[...] = jnp.where(k == 0, upper, low).astype(BF16)
    swap = remote(fs, fr, f_s, f_r, other)
    go(swap)
    out_ref[:, pl.ds(pl.multiple_of(k * HC, HC), HC)] = jnp.where(k == 0, low, upper).astype(BF16)
    swap.wait_recv()
    out_ref[:, pl.ds(pl.multiple_of((1 - k) * HC, HC), HC)] = fr[...]
    for cp in sent:
        cp.wait_send()


def experts(mixed, gain, meta, wo, wg, wu, wd):
    dma = pltpu.SemaphoreType.DMA
    vmem = pl.BlockSpec(memory_space=VMEM)
    hbm = pl.BlockSpec(memory_space=pl.ANY)
    return pl.pallas_call(
        experts_kernel,
        out_shape=jax.ShapeDtypeStruct((4, WIDE), BF16),
        in_specs=[vmem] * 3 + [hbm] * 4,
        out_specs=vmem,
        scratch_shapes=[
            VMEM((256, WIDE), BF16), VMEM((WIDE, FF), BF16), VMEM((WIDE, FF), BF16), VMEM((FF, WIDE), BF16),
            VMEM((2, 2, 16, 8, MSG), BF16), VMEM((16, 8, HC), F32), VMEM((4, 8, HC), F32),
            VMEM((3, 16, 8, HC), BF16), VMEM((3, 16, 8, HC), BF16),
            VMEM((3, 3, 4, 8, HC), BF16), VMEM((3, 3, 4, 8, HC), BF16),
            VMEM((3, 3, 8, HC), BF16), VMEM((3, 3, 8, HC), BF16),
            VMEM((8, HC), BF16), VMEM((8, HC), BF16), VMEM((4, HC), BF16), VMEM((4, HC), BF16),
            VMEM((128, FF), BF16),
            dma((4,)),
            dma((2, 3)), dma((2, 3)), dma((2, 4, 3)), dma((2, 4, 3)), dma((2, 4, 4)), dma((2, 4, 4)),
            dma((3, 3)), dma((3, 3)), dma((3, 3)), dma((3, 3)), dma((3, PARTS)), dma((3, PARTS)),
            dma((2,)), dma((2,)), dma, dma,
        ],
        compiler_params=pltpu.CompilerParams(collective_id=1, has_side_effects=True),
        name="project_experts",
    )(mixed, gain, meta, wo, wg, wu, wd)


def on_device(
    queries, keys, values, out_weight, norm_gain, routes, route_weight, w_gate, w_up, w_down
):
    blocks, lanes, rows, local_heads, head_dim = queries.shape
    e = lax.axis_index("exp")
    y, k = e // 8, lax.rem(e, 2)
    mine = jnp.stack(
        [
            lax.dynamic_index_in_dim(keys, y, 1, keepdims=False),
            lax.dynamic_index_in_dim(values, y, 1, keepdims=False),
        ]
    )
    query_vector = queries.reshape(blocks * rows, local_heads, head_dim).transpose(1, 0, 2)
    mixed = attention(query_vector, mine)
    share = route_weight / jnp.sum(route_weight, axis=1, keepdims=True)
    expert = jnp.arange(128, dtype=jnp.int32)
    expert = jnp.where((expert >= 16) & (expert < 48), expert % 16, -1)
    table = jnp.sum(jnp.where(routes[:, :, None] == expert[None, None, :], share[:, :, None], 0.0), axis=1)
    meta = jnp.where((jnp.arange(8)[:, None] // 4) == k, jnp.concatenate([table, table]), 0.0)
    return experts(mixed, norm_gain[None, :], meta, out_weight, w_gate, w_up, w_down)


def solution(mesh):
    in_specs = (
        P("ctx", "tp", None, "exp", None),
        P("ctx", None, None),
        P("ctx", None, None),
        P("exp", None),
        P(),
        P(("ctx", "exp", "tp"), None),
        P(("ctx", "exp", "tp"), None),
        P("exp", None, "tp"),
        P("exp", None, "tp"),
        P("exp", "tp", None),
    )
    out_specs = P(("ctx", "exp", "tp"), None)
    return jax.shard_map(
        on_device, mesh=mesh, in_specs=in_specs, out_specs=out_specs, check_vma=False
    )
```

```python
import functools
import jax
import jax.numpy as jnp
from jax import lax
from jax.experimental import pallas as pl
from jax.experimental.pallas import tpu as pltpu
from jax.sharding import PartitionSpec as P

MESH = pl.DeviceIdType.MESH
VMEM = pltpu.VMEM
F32 = jnp.float32
BF16 = jnp.bfloat16
CHUNK = 256
HALF = 128
NC = 16


def where_am_i():
    c = lax.axis_index("ctx")
    e = lax.axis_index("exp")
    t = lax.axis_index("tp")
    return t * NC + c, e // 8, lax.rem(e // 2, 4), lax.rem(e, 2)


def device(z, y, x, k):
    z = lax.rem(z + 2 * NC, 2 * NC)
    y = lax.rem(y + 4, 4)
    x = lax.rem(x + 4, 4)
    return (lax.rem(z, NC), (y * 4 + x) * 2 + k, z // NC)


def remote(src, dst, ssem, rsem, dev):
    return pltpu.make_async_remote_copy(
        src_ref=src, dst_ref=dst, send_sem=ssem, recv_sem=rsem, device_id=dev, device_id_type=MESH
    )


WIDE = 4096
HC = 2048
MSG = HC + 128
FF = 192
COLS = 512
PARTS = HC // COLS
NT = (((1,), (1,)), ((), ()))


def when(cond):
    return pl.when(cond)


def layer_kernel(
    routes_ref, weight_ref, gain_ref, q_hbm, k_hbm, v_hbm, wo_hbm, wg_hbm, wu_hbm, wd_hbm, out_ref,
    qv, kin, wide, mine, kv, mx, den, mixacc, pairs,
    wo, wg, wu, wd, xb, acc, keep, s0, r0, s1, r1, s2, r2, xs, xr, fs, fr, first_moe,
    in_sem, hu, hd, up_s, up_r, dn_s, dn_r, x_s, x_r, g_s, g_r,
    b_s, b_r, a_s, a_r, c_s, c_r, m_s, m_r, n_s, n_r, l_s, l_r, z_s, z_r, f_s, f_r,
):
    z, y, x, k = where_am_i()
    c = lax.axis_index("ctx")
    t = lax.axis_index("tp")
    half = lax.rem(x, 2)
    a = x * (1 - k) + y * k
    o = y * (1 - k) + x * k
    other = device(z, y, x, 1 - k)
    beside = device(z, y, x + 1 - 2 * half, k)
    up1, up2 = device(z + 1, y, x, k), device(z + 2, y, x, k)
    dn1, dn2 = device(z - 1, y, x, k), device(z - 2, y, x, k)
    to_a = [None] + [device(z, y + r * k, x + r * (1 - k), k) for r in (1, 2, 3)]
    to_b = [None] + [device(z, y + r * (1 - k), x + r * k, k) for r in (1, 2, 3)]
    far = device(z + jnp.where(lax.rem(z // 8, 2) == 1, 8, -8), y, x, k)

    peers = [up1, up2, dn1, dn2, other] + to_a[1:] + to_b[1:]
    barrier = pltpu.get_barrier_semaphore()
    for d in peers:
        pl.semaphore_signal(barrier, inc=1, device_id=d, device_id_type=MESH)
    loads = [
        pltpu.make_async_copy(src, dst, in_sem.at[i])
        for i, (src, dst) in enumerate(
            (
                (k_hbm, kin.at[0]), (v_hbm, kin.at[1]), (q_hbm, qv), (wo_hbm, wo),
                (wg_hbm.at[0], wg), (wu_hbm.at[0], wu), (wd_hbm.at[0], wd),
            )
        )
    ]
    for cp in loads:
        cp.start()
    sent = []

    def go(cp):
        cp.start()
        sent.append(cp)

    def block(aa, oo):
        aa, oo = lax.rem(aa + 4, 4), lax.rem(oo + 4, 4)
        return oo * (4 - 3 * k) + aa * (1 + 3 * k)

    me = block(a, o)

    def piece(pos):
        return kv.at[k, pos, half]

    def slot_up(d):
        return 2 * (d - 1)

    def slot_dn(d):
        return 2 * (d - 1) + 1

    own = mine.at[k, pl.ds(half * HALF, HALF)]
    ups, dns = [None], [None]
    for d in range(1, 9):
        src = own if d < 3 else piece(slot_up(d - 2))
        ups.append(remote(src, piece(slot_up(d)), up_s.at[d - 1], up_r.at[d - 1], up1 if d == 1 else up2))
    for d in range(1, 8):
        src = own if d < 3 else piece(slot_dn(d - 2))
        dns.append(remote(src, piece(slot_dn(d)), dn_s.at[d - 1], dn_r.at[d - 1], dn1 if d == 1 else dn2))
    xc = [remote(piece(p), piece(p), x_s.at[p], x_r.at[p], beside) for p in range(15)]
    gc = [remote(kv.at[k, p], kv.at[k, p], g_s.at[p], g_r.at[p], other) for p in range(15)]

    def sends_up(d):
        return c + d <= 15 if d < 3 else (c >= d - 2) & (c <= 13)

    def has_up(d):
        return c >= d

    def has_dn(d):
        return lax.rem(c + d, NC) < (7 if d % 2 else 6)

    def sends_dn(d):
        return c < (7 if d == 1 else 6) if d < 3 else has_dn(d - 2)

    def needs_dn(d):
        return c + d >= NC

    loads[0].wait()
    loads[1].wait()
    for i in range(2):
        wide[i] = kin[i].astype(F32)
        mine[i] = wide[i, pl.ds(y, CHUNK, stride=4), :].astype(BF16)
    pl.semaphore_wait(barrier, len(peers))
    when(sends_up(1))(ups[1].start)
    when(sends_dn(1))(dns[1].start)
    when(sends_up(2))(ups[2].start)
    when(sends_dn(2))(dns[2].start)
    pl.semaphore_signal(hu.at[0], inc=1, device_id=up2, device_id_type=MESH)
    pl.semaphore_signal(hd.at[0], inc=1, device_id=dn2, device_id_type=MESH)

    scale = 128 ** (-0.5)
    loads[2].wait()

    def scores(keys):
        return lax.dot_general(qv[...], keys, NT, preferred_element_type=F32) * scale

    def mix(prob, vals):
        return jnp.dot(prob.astype(BF16), vals, preferred_element_type=F32)

    s = scores(mine[0])
    row = lax.broadcasted_iota(jnp.int32, (256, CHUNK), 0) >> 1
    col = lax.broadcasted_iota(jnp.int32, (256, CHUNK), 1)
    ok = col <= ((row >> 2) * 2 + t) * 4 + (row & 3)
    s = jnp.where(ok, s, -1e30)
    m = jnp.max(s, axis=1, keepdims=True)
    e = jnp.where(ok, jnp.exp(s - m), 0.0)
    mx[...] = m
    den[...] = jnp.sum(e, axis=1, keepdims=True)
    mixacc[...] = mix(e, mine[1])

    def z_stage(d):
        @when(has_up(d))
        def _():
            ups[d].wait_recv()
            if d + 2 <= 8:
                when(c <= 13)(ups[d + 2].start)
            xc[slot_up(d)].start()

        if d <= 7:
            @when(has_dn(d))
            def _():
                dns[d].wait_recv()
                if d + 2 <= 7:
                    dns[d + 2].start()
                when(needs_dn(d))(xc[slot_dn(d)].start)

    def x_stage(d):
        @when(has_up(d))
        def _():
            xc[slot_up(d)].wait_recv()
            gc[slot_up(d)].start()

        if d <= 7:
            @when(needs_dn(d))
            def _():
                xc[slot_dn(d)].wait_recv()
                gc[slot_dn(d)].start()

    def absorb_one(p):
        gc[p].wait_recv()
        s = scores(kv[0, p].reshape(CHUNK, 128))
        m = mx[...]
        m_new = jnp.maximum(m, jnp.max(s, axis=1, keepdims=True))
        fade = jnp.exp(m - m_new)
        e = jnp.exp(s - m_new)
        mx[...] = m_new
        den[...] = den[...] * fade + jnp.sum(e, axis=1, keepdims=True)
        mixacc[...] = mixacc[...] * fade + mix(e, kv[1, p].reshape(CHUNK, 128))

    def absorb(d):
        when(has_up(d))(functools.partial(absorb_one, slot_up(d)))
        if d <= 7:
            when(needs_dn(d))(functools.partial(absorb_one, slot_dn(d)))

    def hello(j):
        pl.semaphore_wait(hu.at[j], 1)
        if j < 2:
            pl.semaphore_signal(hu.at[j + 1], inc=1, device_id=up2, device_id_type=MESH)
        pl.semaphore_wait(hd.at[j], 1)
        if j < 2:
            pl.semaphore_signal(hd.at[j + 1], inc=1, device_id=dn2, device_id_type=MESH)

    for i in range(1, 11):
        if i <= 8:
            z_stage(i)
        if 1 <= i - 1 <= 8:
            x_stage(i - 1)
        if i in (3, 5, 8):
            hello({3: 0, 5: 1, 8: 2}[i])
        if 1 <= i - 2 <= 8:
            absorb(i - 2)
    pairs[...] = mixacc[...] / den[...]

    def rs_pair(i, j):
        cols = pl.ds(j * COLS, COLS)
        return remote(s0.at[i, :, :, cols], r0.at[i, :, :, cols], l_s.at[i, j], l_r.at[i, j], other)

    def rs_a(i, r):
        return remote(s1.at[i, r - 1], r1.at[i, r - 1], m_s.at[i, r - 1], m_r.at[i, r - 1], to_a[r])

    def rs_b(i, r):
        return remote(s2.at[i, r - 1], r2.at[i, r - 1], n_s.at[i, r - 1], n_r.at[i, r - 1], to_b[r])

    def times(lhs, w, half, j):
        cols = pl.ds(pl.multiple_of(half * HC + j * COLS, COLS), COLS)
        return jnp.dot(lhs, w[:, cols], preferred_element_type=F32).reshape(16, 8, COLS)

    def rs_pair_fill(i, lhs, w):
        for j in range(PARTS):
            s0[i, :, :, j * COLS:(j + 1) * COLS] = times(lhs, w, 1 - k, j).astype(BF16)

    def rs_pair_go(i):
        for j in range(PARTS):
            go(rs_pair(i, j))

    def rs_own(lhs, w):
        for j in range(PARTS):
            acc[:, :, j * COLS:(j + 1) * COLS] = times(lhs, w, k, j)

    def rs_first(i):
        for j in range(PARTS):
            rs_pair(i, j).wait_recv()
        for r in (2, 1, 3, 0):
            for oo in range(4):
                b = block(a + r, oo)
                v = acc[b] + r0[i, b].astype(F32)
                if r:
                    s1[i, r - 1, oo] = v.astype(BF16)
                else:
                    keep[oo] = v
            if r:
                go(rs_a(i, r))

    def rs_second(i):
        for r in (1, 3, 2):
            rs_a(i, r).wait_recv()
        for r in (2, 1, 3, 0):
            oo = lax.rem(o + r, 4)
            v = keep[oo]
            for q in range(3):
                v = v + r1[i, q, oo].astype(F32)
            if r:
                s2[i, r - 1] = v.astype(BF16)
                go(rs_b(i, r))
        return v

    def rs_last(i, v):
        for r in (1, 3, 2):
            rs_b(i, r).wait_recv()
        for q in range(3):
            v = v + r2[i, q].astype(F32)
        return v

    def ag_b(p, r):
        blk = xb.at[p, k, me]
        return remote(blk, blk, b_s.at[p, r - 1], b_r.at[p, r - 1], to_b[r])

    def ag_a(p, q, r):
        blk = xb.at[p, k, block(a, o - q)]
        return remote(blk, blk, a_s.at[p, q, r - 1], a_r.at[p, q, r - 1], to_a[r])

    def ag_c(p, q, r):
        blk = xb.at[p, k, block(a - r, o - q)]
        return remote(blk, blk, c_s.at[p, q, r], c_r.at[p, q, r], other)

    def ag_start(p):
        for r in (2, 1, 3):
            ag_b(p, r).start()
        for r in (2, 1, 3):
            ag_a(p, 0, r).start()
        ag_c(p, 0, 0).start()

    def ag_forward(p):
        for q in (1, 3, 2):
            ag_b(p, q).wait_recv()
            for r in (2, 1, 3):
                ag_a(p, q, r).start()
            ag_c(p, q, 0).start()

    def ag_pair(p):
        for q in (0, 1, 3, 2):
            for r in (1, 3, 2):
                ag_a(p, q, r).wait_recv()
                ag_c(p, q, r).start()

    def ag_wait(p):
        for q in range(4):
            for r in range(4):
                ag_c(p, q, r).wait_recv()

    lane = lax.broadcasted_iota(jnp.int32, (1, 128), 1)
    expert = lax.rem((y * 4 + x) * 2 + k, 16)

    def ffn_half(p, h, gate, up):
        for j in range(PARTS):
            at = pl.ds(pl.multiple_of(h * HC + j * COLS, COLS), COLS)
            v = xb[p, h, :, :, j * COLS:(j + 1) * COLS].astype(F32).reshape(128, COLS)
            v = (v * gain_ref[:, at]).astype(BF16)
            gate = gate + lax.dot_general(v, wg[:, at], NT, preferred_element_type=F32)
            up = up + lax.dot_general(v, wu[:, at], NT, preferred_element_type=F32)
        return gate, up

    def ffn(p):
        zero = jnp.zeros((128, FF), F32)
        gate, up = ffn_half(p, k, zero, zero)
        ag_wait(p)
        gate, up = ffn_half(p, 1 - k, gate, up)
        info = xb[p, 0, :, :, HC:MSG].astype(F32) + xb[p, 1, :, :, HC:MSG].astype(F32)
        info = info.reshape(128, 128)
        square = jnp.sum(jnp.where(lane < 16, info, 0.0), axis=1, keepdims=True)
        chosen = (lane == 16 + expert) | (lane == 32 + expert)
        share = jnp.sum(jnp.where(chosen, info, 0.0), axis=1, keepdims=True)
        inverse = lax.rsqrt(square * (1.0 / WIDE) + 1e-06)
        gate, up = gate * inverse, up * inverse
        return (gate / (1.0 + jnp.exp(-gate)) * up * share).astype(BF16)

    mixed = jnp.concatenate(
        [pairs[pl.ds(0, 128, stride=2), :], pairs[pl.ds(1, 128, stride=2), :]], axis=1
    ).astype(BF16)
    loads[3].wait()
    rs_pair_fill(0, mixed, wo)
    rs_pair_go(0)
    rs_own(mixed, wo)
    rs_first(0)
    share = weight_ref[...]
    share = share / jnp.sum(share, axis=1, keepdims=True)
    label = jnp.where((lane >= 16) & (lane < 48), lane & 15, -1)
    table = jnp.zeros((4, 128), F32)
    for j in range(8):
        table = table + jnp.where(routes_ref[:, j:j + 1] == label, share[:, j:j + 1], 0.0)
    rows8 = lax.broadcasted_iota(jnp.int32, (8, 128), 0)
    meta = jnp.where((rows8 >> 2) == k, jnp.concatenate([table, table], axis=0), 0.0)
    high = meta.astype(BF16).astype(F32)
    meta = jnp.where(lane < 32, high, meta - high)
    state = rs_last(0, rs_second(0)).astype(BF16)
    state_wide = state.astype(F32)
    square = jnp.sum(state_wide * state_wide, axis=1, keepdims=True)
    top = square.astype(BF16).astype(F32)
    mid = (square - top).astype(BF16).astype(F32)
    info = jnp.where(lane == 0, top, meta)
    info = jnp.where(lane == 1, mid, info)
    info = jnp.where(lane == 2, square - top - mid, info)
    xb[0, k, me, :, 0:HC] = state
    xb[0, k, me, :, HC:MSG] = info.astype(BF16)
    cross = remote(xb.at[0, k, me], xb.at[1, k, me], z_s.at[0], z_r.at[0], far)
    go(cross)
    ag_start(0)
    for cp in loads[4:]:
        cp.wait()
    begin = t

    def enter():
        cross.wait_recv()
        ag_start(1)

    def second():
        ag_forward(0)
        ag_pair(0)

    when(t == 1)(enter)
    ag_forward(begin)
    ag_pair(begin)
    when(t == 1)(second)
    hidden = ffn(begin)
    rs_pair_fill(1, hidden, wd)
    rs_pair_go(1)
    rs_own(hidden, wd)
    when(t == 0)(enter)
    rs_first(1)
    when(t == 0)(functools.partial(ag_forward, 1))
    v = rs_second(1)
    when(t == 0)(functools.partial(ag_pair, 1))
    v = rs_last(1, v)
    first_moe[...] = v
    back = remote(xs, xr, z_s.at[1], z_r.at[1], far)

    @when(t == 1)
    def _():
        xs[...] = v.astype(BF16)
        back.start()

    hidden = ffn(1 - begin)
    rs_pair_fill(2, hidden, wd)
    rs_pair_go(2)
    rs_own(hidden, wd)
    rs_first(2)
    last = rs_last(2, rs_second(2))

    @when(t == 0)
    def _():
        xs[...] = last.astype(BF16)
        back.start()

    moe = jnp.where(t == 0, first_moe[...], last)
    back.wait_recv()
    total = (state_wide + moe + xr[...].astype(F32)).astype(BF16).astype(F32)
    low, upper = total[0:4], total[4:8]
    fs[...] = jnp.where(k == 0, upper, low).astype(BF16)
    swap = remote(fs, fr, f_s, f_r, other)
    swap.start()
    out_ref[:, pl.ds(pl.multiple_of(k * HC, HC), HC)] = jnp.where(k == 0, low, upper).astype(BF16)
    swap.wait_recv()
    out_ref[:, pl.ds(pl.multiple_of((1 - k) * HC, HC), HC)] = fr[...]
    for d in range(1, 9):
        when(sends_up(d))(ups[d].wait_send)
        when(has_up(d))(xc[slot_up(d)].wait_send)
        when(has_up(d))(gc[slot_up(d)].wait_send)
        if d <= 7:
            when(sends_dn(d))(dns[d].wait_send)
            when(needs_dn(d))(xc[slot_dn(d)].wait_send)
            when(needs_dn(d))(gc[slot_dn(d)].wait_send)
    swap.wait_send()
    back.wait_send()
    for p in range(2):
        for q in range(4):
            ag_c(p, q, 0).wait_send()
            for r in (1, 2, 3):
                ag_a(p, q, r).wait_send()
                ag_c(p, q, r).wait_send()
        for r in (1, 2, 3):
            ag_b(p, r).wait_send()
    for cp in sent:
        cp.wait_send()


def layer(routes, weight, gain, q, keys, values, wo, wg, wu, wd):
    dma = pltpu.SemaphoreType.DMA
    vmem = pl.BlockSpec(memory_space=VMEM)
    hbm = pl.BlockSpec(memory_space=pl.ANY)
    return pl.pallas_call(
        layer_kernel,
        out_shape=jax.ShapeDtypeStruct((4, WIDE), BF16),
        in_specs=[vmem] * 3 + [hbm] * 7,
        out_specs=vmem,
        scratch_shapes=[
            VMEM((256, 128), BF16), VMEM((2, 1024, 128), BF16), VMEM((2, 1024, 128), F32),
            VMEM((2, CHUNK, 128), BF16), VMEM((2, 15, 2, HALF, 128), BF16),
            VMEM((256, 1), F32), VMEM((256, 1), F32), VMEM((256, 128), F32), VMEM((256, 128), F32),
            VMEM((256, WIDE), BF16), VMEM((FF, WIDE), BF16), VMEM((FF, WIDE), BF16), VMEM((FF, WIDE), BF16),
            VMEM((2, 2, 16, 8, MSG), BF16), VMEM((16, 8, HC), F32), VMEM((4, 8, HC), F32),
            VMEM((3, 16, 8, HC), BF16), VMEM((3, 16, 8, HC), BF16),
            VMEM((3, 3, 4, 8, HC), BF16), VMEM((3, 3, 4, 8, HC), BF16),
            VMEM((3, 3, 8, HC), BF16), VMEM((3, 3, 8, HC), BF16),
            VMEM((8, HC), BF16), VMEM((8, HC), BF16), VMEM((4, HC), BF16), VMEM((4, HC), BF16),
            VMEM((8, HC), F32),
            dma((7,)), pltpu.SemaphoreType.REGULAR((3,)), pltpu.SemaphoreType.REGULAR((3,)),
            dma((8,)), dma((8,)), dma((7,)), dma((7,)), dma((15,)), dma((15,)), dma((15,)), dma((15,)),
            dma((2, 3)), dma((2, 3)), dma((2, 4, 3)), dma((2, 4, 3)), dma((2, 4, 4)), dma((2, 4, 4)),
            dma((3, 3)), dma((3, 3)), dma((3, 3)), dma((3, 3)), dma((3, PARTS)), dma((3, PARTS)),
            dma((2,)), dma((2,)), dma, dma,
        ],
        compiler_params=pltpu.CompilerParams(collective_id=0, has_side_effects=True),
        name="layer",
    )(routes, weight, gain, q, keys, values, wo, wg, wu, wd)


def on_device(
    queries, keys, values, out_weight, norm_gain, routes, route_weight, w_gate, w_up, w_down
):
    return layer(
        routes, route_weight, norm_gain[None, :],
        queries.reshape(256, 128), keys.reshape(1024, 128), values.reshape(1024, 128),
        out_weight, w_gate.swapaxes(1, 2), w_up.swapaxes(1, 2), w_down,
    )


def solution(mesh):
    in_specs = (
        P("ctx", "tp", None, "exp", None),
        P("ctx", None, None),
        P("ctx", None, None),
        P("exp", None),
        P(),
        P(("ctx", "exp", "tp"), None),
        P(("ctx", "exp", "tp"), None),
        P("exp", None, "tp"),
        P("exp", None, "tp"),
        P("exp", "tp", None),
    )
    out_specs = P(("ctx", "exp", "tp"), None)
    return jax.shard_map(
        on_device, mesh=mesh, in_specs=in_specs, out_specs=out_specs, check_vma=False
    )
```

```python
import functools
import jax
import jax.numpy as jnp
from jax import lax
from jax.experimental import pallas as pl
from jax.experimental.pallas import tpu as pltpu
from jax.sharding import PartitionSpec as P

MESH = pl.DeviceIdType.MESH
VMEM = pltpu.VMEM
F32 = jnp.float32
BF16 = jnp.bfloat16
CHUNK = 256
HALF = 128
NC = 16


def where_am_i():
    c = lax.axis_index("ctx")
    e = lax.axis_index("exp")
    t = lax.axis_index("tp")
    return t * NC + c, e // 8, lax.rem(e // 2, 4), lax.rem(e, 2)


def device(z, y, x, k):
    z = lax.rem(z + 2 * NC, 2 * NC)
    y = lax.rem(y + 4, 4)
    x = lax.rem(x + 4, 4)
    return (lax.rem(z, NC), (y * 4 + x) * 2 + k, z // NC)


def remote(src, dst, ssem, rsem, dev):
    return pltpu.make_async_remote_copy(
        src_ref=src, dst_ref=dst, send_sem=ssem, recv_sem=rsem, device_id=dev, device_id_type=MESH
    )


WIDE = 4096
HC = 2048
MSG = HC + 128
FF = 192
COLS = 512
PARTS = HC // COLS
GC = 1024
SPLIT = GC // COLS
GROUPS = HC // GC
NT = (((1,), (1,)), ((), ()))


def when(cond):
    return pl.when(cond)


def layer_kernel(
    routes_ref, weight_ref, gain_ref, q_hbm, k_hbm, v_hbm, wo_hbm, wg_hbm, wu_hbm, wd_hbm, out_ref,
    qv, kin, wide, mine, kv, mx, den, mixacc, pairs,
    wo, wg, wu, wd, xb, acc, keep, s0, r0, s1, r1, s2, r2, xs, xr, fs, fr, first_moe,
    in_sem, hu, hd, up_s, up_r, dn_s, dn_r, x_s, x_r, g_s, g_r,
    b_s, b_r, a_s, a_r, c_s, c_r, m_s, m_r, n_s, n_r, l_s, l_r, z_s, z_r, f_s, f_r,
):
    z, y, x, k = where_am_i()
    c = lax.axis_index("ctx")
    t = lax.axis_index("tp")
    half = lax.rem(x, 2)
    a = x * (1 - k) + y * k
    o = y * (1 - k) + x * k
    other = device(z, y, x, 1 - k)
    beside = device(z, y, x + 1 - 2 * half, k)
    up1, up2 = device(z + 1, y, x, k), device(z + 2, y, x, k)
    dn1, dn2 = device(z - 1, y, x, k), device(z - 2, y, x, k)
    to_a = [None] + [device(z, y + r * k, x + r * (1 - k), k) for r in (1, 2, 3)]
    to_b = [None] + [device(z, y + r * (1 - k), x + r * k, k) for r in (1, 2, 3)]
    far = device(z + jnp.where(lax.rem(z // 8, 2) == 1, 8, -8), y, x, k)

    peers = [up1, up2, dn1, dn2, other] + to_a[1:] + to_b[1:]
    barrier = pltpu.get_barrier_semaphore()
    for d in peers:
        pl.semaphore_signal(barrier, inc=1, device_id=d, device_id_type=MESH)
    loads = [
        pltpu.make_async_copy(src, dst, in_sem.at[i])
        for i, (src, dst) in enumerate(
            (
                (k_hbm, kin.at[0]), (v_hbm, kin.at[1]), (q_hbm, qv), (wo_hbm, wo),
                (wg_hbm.at[0], wg), (wu_hbm.at[0], wu), (wd_hbm.at[0], wd),
            )
        )
    ]
    for cp in loads:
        cp.start()
    sent = []

    def go(cp):
        cp.start()
        sent.append(cp)

    def block(aa, oo):
        aa, oo = lax.rem(aa + 4, 4), lax.rem(oo + 4, 4)
        return oo * (4 - 3 * k) + aa * (1 + 3 * k)

    me = block(a, o)

    def piece(pos):
        return kv.at[k, pos, half]

    def slot_up(d):
        return 2 * (d - 1)

    def slot_dn(d):
        return 2 * (d - 1) + 1

    own = mine.at[k, pl.ds(half * HALF, HALF)]
    ups, dns = [None], [None]
    for d in range(1, 9):
        src = own if d < 3 else piece(slot_up(d - 2))
        ups.append(remote(src, piece(slot_up(d)), up_s.at[d - 1], up_r.at[d - 1], up1 if d == 1 else up2))
    for d in range(1, 8):
        src = own if d < 3 else piece(slot_dn(d - 2))
        dns.append(remote(src, piece(slot_dn(d)), dn_s.at[d - 1], dn_r.at[d - 1], dn1 if d == 1 else dn2))
    xc = [remote(piece(p), piece(p), x_s.at[p], x_r.at[p], beside) for p in range(15)]
    gc = [remote(kv.at[k, p], kv.at[k, p], g_s.at[p], g_r.at[p], other) for p in range(15)]

    def sends_up(d):
        return c + d <= 15 if d < 3 else (c >= d - 2) & (c <= 13)

    def has_up(d):
        return c >= d

    def has_dn(d):
        return lax.rem(c + d, NC) < (7 if d % 2 else 6)

    def sends_dn(d):
        return c < (7 if d == 1 else 6) if d < 3 else has_dn(d - 2)

    def needs_dn(d):
        return c + d >= NC

    loads[0].wait()
    loads[1].wait()
    for i in range(2):
        wide[i] = kin[i].astype(F32)
        mine[i] = wide[i, pl.ds(y, CHUNK, stride=4), :].astype(BF16)
    pl.semaphore_wait(barrier, len(peers))
    when(sends_up(1))(ups[1].start)
    when(sends_dn(1))(dns[1].start)
    when(sends_up(2))(ups[2].start)
    when(sends_dn(2))(dns[2].start)
    pl.semaphore_signal(hu.at[0], inc=1, device_id=up2, device_id_type=MESH)
    pl.semaphore_signal(hd.at[0], inc=1, device_id=dn2, device_id_type=MESH)

    scale = 128 ** (-0.5)
    loads[2].wait()

    def scores(keys):
        return lax.dot_general(qv[...], keys, NT, preferred_element_type=F32) * scale

    def mix(prob, vals):
        return jnp.dot(prob.astype(BF16), vals, preferred_element_type=F32)

    s = scores(mine[0])
    row = lax.broadcasted_iota(jnp.int32, (256, CHUNK), 0) >> 1
    col = lax.broadcasted_iota(jnp.int32, (256, CHUNK), 1)
    ok = col <= ((row >> 2) * 2 + t) * 4 + (row & 3)
    s = jnp.where(ok, s, -1e30)
    m = jnp.max(s, axis=1, keepdims=True)
    e = jnp.where(ok, jnp.exp(s - m), 0.0)
    mx[...] = m
    den[...] = jnp.sum(e, axis=1, keepdims=True)
    mixacc[...] = mix(e, mine[1])

    def z_stage(d):
        @when(has_up(d))
        def _():
            ups[d].wait_recv()
            if d + 2 <= 8:
                when(c <= 13)(ups[d + 2].start)
            xc[slot_up(d)].start()

        if d <= 7:
            @when(has_dn(d))
            def _():
                dns[d].wait_recv()
                if d + 2 <= 7:
                    dns[d + 2].start()
                when(needs_dn(d))(xc[slot_dn(d)].start)

    def x_stage(d):
        @when(has_up(d))
        def _():
            xc[slot_up(d)].wait_recv()
            gc[slot_up(d)].start()

        if d <= 7:
            @when(needs_dn(d))
            def _():
                xc[slot_dn(d)].wait_recv()
                gc[slot_dn(d)].start()

    def absorb(ds):
        slots = []
        for d in ds:
            slots.append((slot_up(d), has_up(d)))
            if d <= 7:
                slots.append((slot_dn(d), needs_dn(d)))

        @when(has_up(ds[0]))
        def _():
            for p, needed in slots:
                when(needed)(gc[p].wait_recv)
            n = len(slots)
            keys = kv[0, pl.ds(slots[0][0], n)].reshape(n * CHUNK, 128)
            lane = lax.broadcasted_iota(jnp.int32, (1, n * CHUNK), 1)
            valid = jnp.zeros((1, n * CHUNK), jnp.int32)
            vals = []
            for j, (p, needed) in enumerate(slots):
                flag = jnp.where(needed, 1, 0)
                valid = jnp.where((lane >> 8) == j, flag, valid)
                v = kv[1, p].reshape(CHUNK, 128)
                vals.append(jnp.where(flag == 1, v, jnp.zeros_like(v)))
            s = jnp.where(valid == 1, scores(keys), -1e30)
            m = mx[...]
            m_new = jnp.maximum(m, jnp.max(s, axis=1, keepdims=True))
            fade = jnp.exp(m - m_new)
            e = jnp.exp(s - m_new)
            mx[...] = m_new
            den[...] = den[...] * fade + jnp.sum(e, axis=1, keepdims=True)
            mixacc[...] = mixacc[...] * fade + mix(e, jnp.concatenate(vals, axis=0))

    def hello(j):
        pl.semaphore_wait(hu.at[j], 1)
        if j < 2:
            pl.semaphore_signal(hu.at[j + 1], inc=1, device_id=up2, device_id_type=MESH)
        pl.semaphore_wait(hd.at[j], 1)
        if j < 2:
            pl.semaphore_signal(hd.at[j + 1], inc=1, device_id=dn2, device_id_type=MESH)

    for i in range(1, 10):
        if i <= 8:
            z_stage(i)
        if i >= 2:
            x_stage(i - 1)
        if i in (1, 2):
            hello(i - 1)
        if i in (4, 6, 8):
            absorb((i - 3, i - 2))
    absorb((7,))
    absorb((8,))
    pairs[...] = mixacc[...] / den[...]

    def rs_pair(i, j):
        cols = pl.ds(j * COLS, COLS)
        return remote(s0.at[i, :, :, cols], r0.at[i, :, :, cols], l_s.at[i, j], l_r.at[i, j], other)

    def rs_a(i, g, r):
        n = (i, g, r - 1)
        return remote(s1.at[n], r1.at[n], m_s.at[n], m_r.at[n], to_a[r])

    def rs_b(i, g, r):
        n = (i, g, r - 1)
        return remote(s2.at[n], r2.at[n], n_s.at[n], n_r.at[n], to_b[r])

    def times(lhs, w, half, j):
        cols = pl.ds(pl.multiple_of(half * HC + j * COLS, COLS), COLS)
        return jnp.dot(lhs, w[:, cols], preferred_element_type=F32).reshape(16, 8, COLS)

    def rs_pair_send(i, lhs, w):
        for j in range(PARTS):
            s0[i, :, :, j * COLS:(j + 1) * COLS] = times(lhs, w, 1 - k, j).astype(BF16)
            go(rs_pair(i, j))

    def rs_first(i, g, lhs, w):
        for j in range(g * SPLIT, (g + 1) * SPLIT):
            acc[:, :, j * COLS:(j + 1) * COLS] = times(lhs, w, k, j)
        for j in range(g * SPLIT, (g + 1) * SPLIT):
            rs_pair(i, j).wait_recv()
        cols = slice(g * GC, (g + 1) * GC)
        for r in (2, 1, 3, 0):
            for oo in range(4):
                b = block(a + r, oo)
                v = acc[b, :, cols] + r0[i, b, :, cols].astype(F32)
                if r:
                    s1[i, g, r - 1, oo] = v.astype(BF16)
                else:
                    keep[oo, :, cols] = v
            if r:
                go(rs_a(i, g, r))

    def rs_second(i, g):
        for r in (1, 3, 2):
            rs_a(i, g, r).wait_recv()
        cols = slice(g * GC, (g + 1) * GC)
        for r in (2, 1, 3, 0):
            oo = lax.rem(o + r, 4)
            v = keep[oo, :, cols]
            for q in range(3):
                v = v + r1[i, g, q, oo].astype(F32)
            if r:
                s2[i, g, r - 1] = v.astype(BF16)
                go(rs_b(i, g, r))
        return v

    def rs_last(i, g, v):
        for r in (1, 3, 2):
            rs_b(i, g, r).wait_recv()
        for q in range(3):
            v = v + r2[i, g, q].astype(F32)
        return v

    def ag_b(p, r):
        blk = xb.at[p, k, me]
        return remote(blk, blk, b_s.at[p, r - 1], b_r.at[p, r - 1], to_b[r])

    def ag_a(p, q, r):
        blk = xb.at[p, k, block(a, o - q)]
        return remote(blk, blk, a_s.at[p, q, r - 1], a_r.at[p, q, r - 1], to_a[r])

    def ag_c(p, q, r):
        blk = xb.at[p, k, block(a - r, o - q)]
        return remote(blk, blk, c_s.at[p, q, r], c_r.at[p, q, r], other)

    def ag_start(p):
        for r in (2, 1, 3):
            ag_b(p, r).start()
        for r in (2, 1, 3):
            ag_a(p, 0, r).start()
        ag_c(p, 0, 0).start()

    def ag_forward(p):
        for q in (1, 3, 2):
            ag_b(p, q).wait_recv()
            for r in (2, 1, 3):
                ag_a(p, q, r).start()
            ag_c(p, q, 0).start()

    def ag_pair(p):
        for q in (0, 1, 3, 2):
            for r in (1, 3, 2):
                ag_a(p, q, r).wait_recv()
                ag_c(p, q, r).start()

    def ag_wait(p):
        for q in range(4):
            for r in range(4):
                ag_c(p, q, r).wait_recv()

    lane = lax.broadcasted_iota(jnp.int32, (1, 128), 1)
    expert = lax.rem((y * 4 + x) * 2 + k, 16)

    def ffn_half(p, h, gate, up):
        for j in range(PARTS):
            at = pl.ds(pl.multiple_of(h * HC + j * COLS, COLS), COLS)
            v = xb[p, h, :, :, j * COLS:(j + 1) * COLS].astype(F32).reshape(128, COLS)
            v = (v * gain_ref[:, at]).astype(BF16)
            gate = gate + lax.dot_general(v, wg[:, at], NT, preferred_element_type=F32)
            up = up + lax.dot_general(v, wu[:, at], NT, preferred_element_type=F32)
        return gate, up

    def ffn(p):
        zero = jnp.zeros((128, FF), F32)
        gate, up = ffn_half(p, k, zero, zero)
        ag_wait(p)
        gate, up = ffn_half(p, 1 - k, gate, up)
        info = xb[p, 0, :, :, HC:MSG].astype(F32) + xb[p, 1, :, :, HC:MSG].astype(F32)
        info = info.reshape(128, 128)
        square = jnp.sum(jnp.where(lane < 16, info, 0.0), axis=1, keepdims=True)
        chosen = (lane == 16 + expert) | (lane == 32 + expert)
        share = jnp.sum(jnp.where(chosen, info, 0.0), axis=1, keepdims=True)
        inverse = lax.rsqrt(square * (1.0 / WIDE) + 1e-06)
        gate, up = gate * inverse, up * inverse
        return (gate / (1.0 + jnp.exp(-gate)) * up * share).astype(BF16)

    late = c >= 8
    early = c < 8
    begin = jnp.where(late, 1, 0)
    cross = remote(xb.at[0, k, me], xb.at[1, k, me], z_s.at[0], z_r.at[0], far)

    def enter():
        cross.wait_recv()
        ag_start(1)

    mixed = jnp.concatenate(
        [pairs[pl.ds(0, 128, stride=2), :], pairs[pl.ds(1, 128, stride=2), :]], axis=1
    ).astype(BF16)
    loads[3].wait()
    rs_pair_send(0, mixed, wo)
    for g in range(GROUPS):
        rs_first(0, g, mixed, wo)
    share = weight_ref[...]
    share = share / jnp.sum(share, axis=1, keepdims=True)
    label = jnp.where((lane >= 16) & (lane < 48), lane & 15, -1)
    table = jnp.zeros((4, 128), F32)
    for j in range(8):
        table = table + jnp.where(routes_ref[:, j:j + 1] == label, share[:, j:j + 1], 0.0)
    rows8 = lax.broadcasted_iota(jnp.int32, (8, 128), 0)
    meta = jnp.where((rows8 >> 2) == k, jnp.concatenate([table, table], axis=0), 0.0)
    high = meta.astype(BF16).astype(F32)
    meta = jnp.where(lane < 32, high, meta - high)
    halves = [rs_second(0, g) for g in range(GROUPS)]
    state = jnp.concatenate([rs_last(0, g, halves[g]) for g in range(GROUPS)], axis=1).astype(BF16)
    state_wide = state.astype(F32)
    square = jnp.sum(state_wide * state_wide, axis=1, keepdims=True)
    top = square.astype(BF16).astype(F32)
    mid = (square - top).astype(BF16).astype(F32)
    info = jnp.where(lane == 0, top, meta)
    info = jnp.where(lane == 1, mid, info)
    info = jnp.where(lane == 2, square - top - mid, info)
    xb[0, k, me, :, 0:HC] = state
    xb[0, k, me, :, HC:MSG] = info.astype(BF16)
    hello(2)
    go(cross)
    ag_start(0)
    for cp in loads[4:]:
        cp.wait()
    when(late)(enter)
    ag_forward(begin)
    ag_pair(begin)
    hidden = ffn(begin)
    rs_pair_send(1, hidden, wd)
    for g in range(GROUPS):
        rs_first(1, g, hidden, wd)
    when(early)(enter)
    halves = [rs_second(1, g) for g in range(GROUPS)]
    ag_forward(1 - begin)
    v = jnp.concatenate([rs_last(1, g, halves[g]) for g in range(GROUPS)], axis=1)
    first_moe[...] = v
    back = remote(xs, xr, z_s.at[1], z_r.at[1], far)

    @when(late)
    def _():
        xs[...] = v.astype(BF16)
        back.start()

    ag_pair(1 - begin)
    hidden = ffn(1 - begin)
    rs_pair_send(2, hidden, wd)
    for g in range(GROUPS):
        rs_first(2, g, hidden, wd)
    halves = [rs_second(2, g) for g in range(GROUPS)]
    last = jnp.concatenate([rs_last(2, g, halves[g]) for g in range(GROUPS)], axis=1)

    @when(early)
    def _():
        xs[...] = last.astype(BF16)
        back.start()

    moe = jnp.where(early, first_moe[...], last)
    back.wait_recv()
    total = (state_wide + moe + xr[...].astype(F32)).astype(BF16).astype(F32)
    low, upper = total[0:4], total[4:8]
    fs[...] = jnp.where(k == 0, upper, low).astype(BF16)
    swap = remote(fs, fr, f_s, f_r, other)
    swap.start()
    out_ref[:, pl.ds(pl.multiple_of(k * HC, HC), HC)] = jnp.where(k == 0, low, upper).astype(BF16)
    swap.wait_recv()
    out_ref[:, pl.ds(pl.multiple_of((1 - k) * HC, HC), HC)] = fr[...]
    for d in range(1, 9):
        when(sends_up(d))(ups[d].wait_send)
        when(has_up(d))(xc[slot_up(d)].wait_send)
        when(has_up(d))(gc[slot_up(d)].wait_send)
        if d <= 7:
            when(sends_dn(d))(dns[d].wait_send)
            when(needs_dn(d))(xc[slot_dn(d)].wait_send)
            when(needs_dn(d))(gc[slot_dn(d)].wait_send)
    swap.wait_send()
    back.wait_send()
    for p in range(2):
        for q in range(4):
            ag_c(p, q, 0).wait_send()
            for r in (1, 2, 3):
                ag_a(p, q, r).wait_send()
                ag_c(p, q, r).wait_send()
        for r in (1, 2, 3):
            ag_b(p, r).wait_send()
    for cp in sent:
        cp.wait_send()


def layer(routes, weight, gain, q, keys, values, wo, wg, wu, wd):
    dma = pltpu.SemaphoreType.DMA
    vmem = pl.BlockSpec(memory_space=VMEM)
    hbm = pl.BlockSpec(memory_space=pl.ANY)
    return pl.pallas_call(
        layer_kernel,
        out_shape=jax.ShapeDtypeStruct((4, WIDE), BF16),
        in_specs=[vmem] * 3 + [hbm] * 7,
        out_specs=vmem,
        scratch_shapes=[
            VMEM((256, 128), BF16), VMEM((2, 1024, 128), BF16), VMEM((2, 1024, 128), F32),
            VMEM((2, CHUNK, 128), BF16), VMEM((2, 15, 2, HALF, 128), BF16),
            VMEM((256, 1), F32), VMEM((256, 1), F32), VMEM((256, 128), F32), VMEM((256, 128), F32),
            VMEM((256, WIDE), BF16), VMEM((FF, WIDE), BF16), VMEM((FF, WIDE), BF16), VMEM((FF, WIDE), BF16),
            VMEM((2, 2, 16, 8, MSG), BF16), VMEM((16, 8, HC), F32), VMEM((4, 8, HC), F32),
            VMEM((3, 16, 8, HC), BF16), VMEM((3, 16, 8, HC), BF16),
            VMEM((3, GROUPS, 3, 4, 8, GC), BF16), VMEM((3, GROUPS, 3, 4, 8, GC), BF16),
            VMEM((3, GROUPS, 3, 8, GC), BF16), VMEM((3, GROUPS, 3, 8, GC), BF16),
            VMEM((8, HC), BF16), VMEM((8, HC), BF16), VMEM((4, HC), BF16), VMEM((4, HC), BF16),
            VMEM((8, HC), F32),
            dma((7,)), pltpu.SemaphoreType.REGULAR((3,)), pltpu.SemaphoreType.REGULAR((3,)),
            dma((8,)), dma((8,)), dma((7,)), dma((7,)), dma((15,)), dma((15,)), dma((15,)), dma((15,)),
            dma((2, 3)), dma((2, 3)), dma((2, 4, 3)), dma((2, 4, 3)), dma((2, 4, 4)), dma((2, 4, 4)),
            dma((3, GROUPS, 3)), dma((3, GROUPS, 3)), dma((3, GROUPS, 3)), dma((3, GROUPS, 3)), dma((3, PARTS)), dma((3, PARTS)),
            dma((2,)), dma((2,)), dma, dma,
        ],
        compiler_params=pltpu.CompilerParams(collective_id=0, has_side_effects=True),
        name="layer",
    )(routes, weight, gain, q, keys, values, wo, wg, wu, wd)


def on_device(
    queries, keys, values, out_weight, norm_gain, routes, route_weight, w_gate, w_up, w_down
):
    return layer(
        routes, route_weight, norm_gain[None, :],
        queries.reshape(256, 128), keys.reshape(1024, 128), values.reshape(1024, 128),
        out_weight, w_gate.swapaxes(1, 2), w_up.swapaxes(1, 2), w_down,
    )


def solution(mesh):
    in_specs = (
        P("ctx", "tp", None, "exp", None),
        P("ctx", None, None),
        P("ctx", None, None),
        P("exp", None),
        P(),
        P(("ctx", "exp", "tp"), None),
        P(("ctx", "exp", "tp"), None),
        P("exp", None, "tp"),
        P("exp", None, "tp"),
        P("exp", "tp", None),
    )
    out_specs = P(("ctx", "exp", "tp"), None)
    return jax.shard_map(
        on_device, mesh=mesh, in_specs=in_specs, out_specs=out_specs, check_vma=False
    )
```
